512 devices in a mesh: pair: 64 (over z, x, core), slab: 8 (over y).
Axes of the slice: x: 4, y: 8, z: 8, core: 2. Of those that a mesh axis runs over, the one named last changes fastest.
Arguments:
- amps: bfloat16 [1024, 1024, 128], P(('pair', 'slab')), may hold values from -6 to 6
- symmetry: int32 [1024], replicated, may hold values from 0 to 3
- screen: int32 [64, 16, 16], P('pair'), may hold values 0 or 1
- owner: int32 [1024], replicated, may hold values from 0 to 63, as said below
- integrals: bfloat16 [64, 2048, 2048], P('pair', 'slab'), may hold values from -0.25 to 0.25
Outputs:
- residual: bfloat16 [1024, 64, 16, 128], P(('pair', 'slab'))
The draws below stay inside these ranges and needn't reach their ends.
Inputs may be any that keep to these rules, and one draw needn't show every extreme that they name: Every owner from 0 to 63 holds exactly 16 tiles.
All inputs are finite; a program needn't handle non-finite values. No bound on the sum of `screen` on one device may be relied on, other than what follows from the above.
Results may differ from the reference program's by a relative error of at most 0.001.
Values may be sent and summed in bfloat16 or wider, within the bound.
A program may use at most 64 MiB of HBM per device.

```python
import math
import jax
import jax.numpy as jnp
import numpy as np
from jax import lax

PT = 128
TILE_DEV = 16
NSYM = 4
NT = 1024
KD = 2048
OCCP = 1024
N_PAIR = 64


def draw_owner(key, part):
    return (jax.random.permutation(key, NT) // TILE_DEV).astype(jnp.int32)


def touch_ends(entries, rng, least, largest):
    index_at = [jax.random.randint(jax.random.fold_in(rng, axis), (), 0, length) for axis, length in enumerate(entries.shape)]
    longest = entries.shape.index(max(entries.shape))
    beside = index_at[:longest] + [(index_at[longest] + 1) % entries.shape[longest]] + index_at[longest + 1:]
    return entries.at[tuple(index_at)].set(least).at[tuple(beside)].set(largest)


def level_of(stream_key, extent, cuts, low, largest):
    factor_of = 1.0
    for dim, shards_of in cuts:
        steps = jax.random.uniform(jax.random.fold_in(jax.random.fold_in(stream_key, 6), dim), (shards_of,), jnp.float32, low / len(cuts), largest / len(cuts))
        factor_of = factor_of * jnp.repeat(jnp.exp(steps), extent[dim] // shards_of).reshape((-1,) + (1,) * (len(extent) - 1 - dim))
    return factor_of


def cumulative_ranks(count, lean):
    portions = [(1 << 20) // math.isqrt(standing ** lean) + 1 for standing in range(1, count + 1)]
    spread = 1 + sum(portions) // (1 << 30)
    return np.cumsum(np.array([max(1, weight // spread) for weight in portions]))


def skewed_ids(rng, extent, count, lean):
    grid = cumulative_ranks(count, lean)
    ticket = jax.random.randint(jax.random.fold_in(rng, 1), extent, 0, int(grid[count - 1]))
    grade = jnp.searchsorted(jnp.asarray(grid, jnp.int32), ticket, side="right")
    return jax.random.permutation(jax.random.fold_in(rng, 2), count)[grade].astype(jnp.int32)


def scatter_about(rng, shape, spread, reach, shards=(), kind=jnp.bfloat16):
    factor_of = level_of(rng, shape, shards, -0.22, 0.18) if shards else 1.0
    drawn = jax.random.normal(rng, shape, jnp.float32) * spread * factor_of
    return jnp.minimum(jnp.maximum(drawn, -reach), reach).astype(kind)


def setup_inputs(seed: int = 0) -> dict:
    keys = jax.random.split(jax.random.key(seed), 6)
    return {
        "amps": scatter_about(keys[0], (OCCP, NT, PT), 1.0, 6.0, ((0, 512),)),
        "symmetry": touch_ends(skewed_ids(keys[1], (NT,), NSYM, 2), jax.random.fold_in(keys[1], 3), 0, NSYM - 1).astype(jnp.int32),
        "screen": touch_ends((jax.random.randint(keys[2], (N_PAIR, TILE_DEV, TILE_DEV), 0, 4) < 3).astype(jnp.int32), jax.random.fold_in(keys[2], 1), 0, 1),
        "owner": draw_owner(jax.random.fold_in(keys[5], 71), 0),
        "integrals": scatter_about(keys[4], (N_PAIR, KD, KD), (KD // 4) ** -0.5, 0.25, ((0, 64), (1, 8))),
    }


def reference(amps, symmetry, screen, owner, integrals):
    tile_order = jnp.argsort(owner, stable=True).astype(jnp.int32).reshape(N_PAIR, TILE_DEV)
    labels = jnp.take(symmetry, tile_order)
    allowed = ((labels[:, :, None] == labels[:, None, :]) & (screen == 1)).astype(jnp.bfloat16)

    def one_owner(owner_index):
        owned = lax.dynamic_index_in_dim(tile_order, owner_index, 0, keepdims=False)
        gathered = jnp.take(amps, owned, axis=1).reshape(OCCP, KD)
        mask_rows = jnp.repeat(lax.dynamic_index_in_dim(allowed, owner_index, 0, keepdims=False), PT, axis=0)
        block_rows = lax.dynamic_index_in_dim(integrals, owner_index, 0, keepdims=False)
        masked = (block_rows.reshape(KD, TILE_DEV, PT) * mask_rows[:, :, None]).reshape(KD, KD)
        return jnp.dot(gathered, masked, preferred_element_type=jnp.float32).astype(jnp.bfloat16)

    blocks = lax.map(one_owner, jnp.arange(N_PAIR, dtype=jnp.int32))
    return jnp.transpose(blocks, (1, 0, 2)).reshape(OCCP, N_PAIR, TILE_DEV, PT)
```

```python
import functools

import jax
import jax.numpy as jnp
from jax import lax
from jax.experimental import pallas as pl
from jax.experimental.pallas import tpu as pltpu
from jax.sharding import PartitionSpec as P

MESH = pl.DeviceIdType.MESH
CHUNKS = 4


def one_hot_bf16(cond):
    return jnp.where(cond, 1.0, 0.0).astype(jnp.bfloat16)


def kernel(
    n_pair,
    n_slab,
    owner_ref,
    sym_ref,
    screen_ref,
    amps_ref,
    b_ref,
    out_ref,
    send_a,
    recv_a,
    a_mat,
    f32_buf,
    gathered,
    mask_ref,
    send_c,
    ring_send,
    ring_recv,
    a_send,
    a_recv,
    c_send,
    c_recv,
):
    pair = lax.axis_index("pair")
    slab = lax.axis_index("slab")
    rows, tiles, width = amps_ref.shape
    per = tiles // n_pair
    depth, cols = b_ref.shape
    chunk = cols // CHUNKS
    up = lax.rem(slab + 1, n_slab)
    down = lax.rem(slab + n_slab - 1, n_slab)
    toward = ((up, 1), (down, -1))

    barrier = pltpu.get_barrier_semaphore()

    @pl.loop(1, n_pair)
    def _(i):
        other = lax.rem(pair + i, n_pair)
        pl.semaphore_signal(barrier, inc=1, device_id=(other, slab), device_id_type=MESH)

    for there, _ in toward:
        pl.semaphore_signal(barrier, inc=1, device_id=(pair, there), device_id_type=MESH)
    pl.semaphore_wait(barrier, n_pair - 1 + 2)

    half = n_slab // 2

    def steps_of(c, way):
        return half if (c + way) % 2 == 0 else half - 1

    def hop(step, c, way):
        there, sign = toward[way]
        block = lax.rem(slab - sign * step + n_slab, n_slab)
        src = b_ref.at[:, pl.ds(c * chunk, chunk)] if step == 0 else gathered.at[block, c]
        return pltpu.make_async_remote_copy(
            src_ref=src,
            dst_ref=gathered.at[block, c],
            send_sem=ring_send.at[way, step, c],
            recv_sem=ring_recv.at[way, step, c],
            device_id=(pair, there),
            device_id_type=MESH,
        )

    def advance(step):
        for c in range(CHUNKS):
            for way in range(2):
                if step < steps_of(c, way):
                    if step:
                        hop(step - 1, c, way).wait_recv()
                    hop(step, c, way).start()

    advance(0)
    for c in range(CHUNKS):
        gathered[slab, c] = b_ref[:, c * chunk : (c + 1) * chunk]

    owned = owner_ref[...]
    sel = lax.broadcasted_iota(jnp.int32, (n_pair, tiles), 0) == owned
    sel_bf = one_hot_bf16(sel)
    count = jnp.zeros((n_pair, tiles), jnp.float32)
    span = 256
    for part in range(tiles // span):
        before = lax.broadcasted_iota(jnp.int32, (span, tiles), 0) + part * span < lax.broadcasted_iota(
            jnp.int32, (span, tiles), 1
        )
        count += jnp.dot(
            sel_bf[:, part * span : (part + 1) * span], one_hot_bf16(before), preferred_element_type=jnp.float32
        )
    base = (lax.broadcasted_iota(jnp.int32, (n_pair, tiles), 0) * per).astype(jnp.float32)
    rank = jnp.sum(jnp.where(sel, count + base, 0.0), axis=0, keepdims=True).astype(jnp.int32)

    flat = jnp.concatenate([amps_ref[o] for o in range(rows)], axis=1)
    for part in range(tiles // span):
        pick = one_hot_bf16(lax.broadcasted_iota(jnp.int32, (span, tiles), 0) + part * span == rank)
        got = jnp.dot(pick, flat, preferred_element_type=jnp.float32).astype(jnp.bfloat16)
        first = part * span // per
        for o in range(rows):
            send_a[first : first + span // per, o] = got[:, o * width : (o + 1) * width].reshape(
                span // per, per, width
            )

    def a_copy(i):
        other = lax.rem(pair + i, n_pair)
        return pltpu.make_async_remote_copy(
            src_ref=send_a.at[other],
            dst_ref=recv_a.at[pair],
            send_sem=a_send,
            recv_sem=a_recv,
            device_id=(other, slab),
            device_id_type=MESH,
        )

    @pl.loop(1, n_pair)
    def _(i):
        a_copy(i).start()

    recv_a[pair] = send_a[pair]

    mine = one_hot_bf16(lax.broadcasted_iota(jnp.int32, (per, tiles), 0) + pair * per == rank)
    classes = lax.broadcasted_iota(jnp.int32, (128, tiles), 0) == sym_ref[...]
    labels = lax.dot_general(
        mine, one_hot_bf16(classes), (((1,), (1,)), ((), ())), preferred_element_type=jnp.float32
    ).astype(jnp.bfloat16)
    same = lax.dot_general(labels, labels, (((1,), (1,)), ((), ())), preferred_element_type=jnp.float32)
    allowed = jnp.where(screen_ref[...] == 1, same, 0.0).astype(jnp.bfloat16)
    spread = one_hot_bf16(
        lax.broadcasted_iota(jnp.int32, (per, cols), 0) == lax.broadcasted_iota(jnp.int32, (per, cols), 1) // width
    )
    mask_ref[...] = jnp.dot(allowed, spread, preferred_element_type=jnp.float32)

    for step in range(1, half):
        advance(step)

    def all_of(ref, sem):
        part = ref.at[pl.ds(0, n_pair - 1)]
        return pltpu.make_async_copy(part, part, sem)

    all_of(recv_a, a_recv).wait()
    f32_buf[...] = recv_a[...].reshape(n_pair * rows * per, width).astype(jnp.float32)
    held = n_pair * rows
    for k in range(per):
        a_mat[:, k * width : (k + 1) * width] = f32_buf[pl.ds(k, held, stride=per), :].astype(jnp.bfloat16)

    for c in range(CHUNKS):
        for way in range(2):
            hop(steps_of(c, way) - 1, c, way).wait_recv()
        acc = None
        for y in range(n_slab):
            term = []
            for part in range(depth // width):
                k = y * (depth // width) + part
                row = mask_ref[k : k + 1, c * chunk : (c + 1) * chunk].astype(jnp.bfloat16)
                term.append(gathered[y, c, part * width : (part + 1) * width, :] * row)
            prod = jnp.dot(
                a_mat[:, y * depth : (y + 1) * depth],
                jnp.concatenate(term, axis=0),
                preferred_element_type=jnp.float32,
            )
            acc = prod if acc is None else acc + prod
        for part in range(chunk // width):
            l = c * (chunk // width) + part
            f32_buf[pl.ds(l, held, stride=per), :] = acc[:, part * width : (part + 1) * width]

    send_c[...] = f32_buf[...].astype(jnp.bfloat16).reshape(n_pair, rows, per, width)

    def c_copy(i):
        other = lax.rem(pair + i, n_pair)
        return pltpu.make_async_remote_copy(
            src_ref=send_c.at[other],
            dst_ref=out_ref.at[:, pair],
            send_sem=c_send,
            recv_sem=c_recv,
            device_id=(other, slab),
            device_id_type=MESH,
        )

    @pl.loop(1, n_pair)
    def _(i):
        c_copy(i).start()

    out_ref[:, pair] = send_c[pair]

    for step in range(half):
        for c in range(CHUNKS):
            for way in range(2):
                if step < steps_of(c, way):
                    hop(step, c, way).wait_send()
    all_of(send_a, a_send).wait()
    all_of(send_c, c_send).wait()
    all_of(send_c, c_recv).wait()


def on_device(amps, symmetry, screen, owner, integrals):
    n_pair, n_slab = lax.axis_size("pair"), lax.axis_size("slab")
    rows, tiles, width = amps.shape
    per = tiles // n_pair
    depth, cols = integrals.shape[1:]
    bf16 = jnp.bfloat16
    vmem = pl.BlockSpec(memory_space=pltpu.VMEM)
    return pl.pallas_call(
        functools.partial(kernel, n_pair, n_slab),
        out_shape=jax.ShapeDtypeStruct((rows, n_pair, per, width), bf16),
        in_specs=[vmem] * 5,
        out_specs=vmem,
        scratch_shapes=[
            pltpu.VMEM((n_pair, rows, per, width), bf16),
            pltpu.VMEM((n_pair, rows, per, width), bf16),
            pltpu.VMEM((n_pair * rows, per * width), bf16),
            pltpu.VMEM((n_pair * rows * per, width), jnp.float32),
            pltpu.VMEM((n_slab, CHUNKS, depth, cols // CHUNKS), bf16),
            pltpu.VMEM((per, cols), jnp.float32),
            pltpu.VMEM((n_pair, rows, per, width), bf16),
            pltpu.SemaphoreType.DMA((2, n_slab // 2, CHUNKS)),
            pltpu.SemaphoreType.DMA((2, n_slab // 2, CHUNKS)),
            pltpu.SemaphoreType.DMA,
            pltpu.SemaphoreType.DMA,
            pltpu.SemaphoreType.DMA,
            pltpu.SemaphoreType.DMA,
        ],
        compiler_params=pltpu.CompilerParams(
            collective_id=0, has_side_effects=True, vmem_limit_bytes=40 << 20
        ),
    )(owner[None, :], symmetry[None, :], screen[0], amps, integrals[0])


def solution(mesh):
    in_specs = (
        P(("pair", "slab"), None, None),
        P(),
        P("pair", None, None),
        P(),
        P("pair", "slab", None),
    )
    out_specs = P(("pair", "slab"), None, None, None)
    return jax.shard_map(
        on_device, mesh=mesh, in_specs=in_specs, out_specs=out_specs, check_vma=False
    )
```

```python
import functools

import jax
import jax.numpy as jnp
from jax import lax
from jax.experimental import pallas as pl
from jax.experimental.pallas import tpu as pltpu
from jax.sharding import PartitionSpec as P

MESH = pl.DeviceIdType.MESH
CORES = 2
RING = 4
ROW = CORES * RING
RELAY = 128


def one_hot_bf16(cond):
    return jnp.where(cond, 1.0, 0.0).astype(jnp.bfloat16)


def kernel(
    n_pair,
    n_slab,
    owner_hbm,
    sym_hbm,
    screen_hbm,
    amps_hbm,
    b_hbm,
    out_ref,
    owner_ref,
    sym_ref,
    screen_ref,
    amps_ref,
    send_a,
    recv_a,
    a_mat,
    f32_buf,
    acc,
    gathered,
    coupling,
    mask_ref,
    send_c,
    load_sem,
    first_send,
    first_recv,
    side_send,
    side_recv,
    relay_send,
    relay_recv,
    twin_send,
    twin_recv,
    screen_send,
    screen_recv,
    a_send,
    a_recv,
    c_send,
    c_recv,
):
    pair = lax.axis_index("pair")
    slab = lax.axis_index("slab")
    rows, tiles, width = amps_hbm.shape
    per = tiles // n_pair
    depth, cols = b_hbm.shape
    piece = cols // ROW
    layer = pair // ROW
    ring = lax.rem(pair // CORES, RING)
    core = lax.rem(pair, CORES)
    row_base = layer * ROW

    home = ring + RING * core
    served = row_base + lax.rem(slab, RING) * CORES + slab // RING
    spot = layer * n_slab + slab

    loads = [
        pltpu.make_async_copy(src, dst, load_sem.at[i])
        for i, (src, dst) in enumerate(
            ((owner_hbm, owner_ref), (sym_hbm, sym_ref), (screen_hbm, screen_ref), (amps_hbm, amps_ref))
        )
    ]
    for load in loads:
        load.start()

    def in_row(i):
        return row_base + lax.rem(pair - row_base + i, ROW)

    def spread_over(i):
        other = lax.rem(spot + i, n_pair)
        there = other // n_slab
        return there * ROW + pair - row_base, lax.rem(other, n_slab)

    barrier = pltpu.get_barrier_semaphore()

    @pl.loop(1, n_pair)
    def _(i):
        pl.semaphore_signal(barrier, inc=1, device_id=spread_over(i), device_id_type=MESH)

    @pl.loop(1, ROW)
    def _(i):
        pl.semaphore_signal(barrier, inc=1, device_id=(in_row(i), slab), device_id_type=MESH)

    @pl.loop(1, n_slab)
    def _(i):
        pl.semaphore_signal(barrier, inc=1, device_id=(served, lax.rem(slab + i, n_slab)), device_id_type=MESH)

    at_home = home == slab

    peers = n_pair - 1 + ROW - 1 + ROW - 1

    @pl.when(at_home)
    def _():
        pl.semaphore_wait(barrier, peers)

    @pl.when(jnp.logical_not(at_home))
    def _():
        pl.semaphore_signal(barrier, inc=1, device_id=(served, slab), device_id_type=MESH)
        pl.semaphore_wait(barrier, peers + 1)

    def first_copy(i):
        other = in_row(i)
        q = other - row_base
        return pltpu.make_async_remote_copy(
            src_ref=b_hbm.at[:, pl.ds(pl.multiple_of(q * piece, piece), piece)],
            dst_ref=gathered.at[slab, q],
            send_sem=first_send,
            recv_sem=first_recv.at[slab],
            device_id=(other, home),
            device_id_type=MESH,
        )

    me = pair - row_base
    own_piece = pltpu.make_async_copy(
        b_hbm.at[:, pl.ds(pl.multiple_of(me * piece, piece), piece)], gathered.at[slab, me], first_recv.at[slab]
    )

    @pl.loop(1, ROW)
    def _(i):
        first_copy(i).start()

    @pl.when(at_home)
    def _():
        own_piece.start()

    @pl.when(jnp.logical_not(at_home))
    def _():
        first_copy(0).start()

    right = row_base + lax.rem(ring + 1, RING) * CORES + core
    left = row_base + lax.rem(ring + RING - 1, RING) * CORES + core
    twin = row_base + ring * CORES + 1 - core
    q_me = me
    q_right, q_left = right - row_base, left - row_base
    q_far = lax.rem(ring + 2, RING) * CORES + core
    order = [0]
    for k in range(1, n_slab // 2):
        order += [k, n_slab - k]
    order += [n_slab // 2]

    def source_of(t):
        return lax.rem(slab + order[t], n_slab)

    def remote(ref, send, recv, to):
        return pltpu.make_async_remote_copy(
            src_ref=ref, dst_ref=ref, send_sem=send, recv_sem=recv, device_id=(to, slab), device_id_type=MESH
        )

    def side(t, way):
        y = source_of(t)
        return remote(gathered.at[y, q_me], side_send.at[way, t], side_recv.at[way, t], (right, left)[way])

    def relay(t, way):
        y = source_of(t)
        part = pl.ds(0, RELAY) if way == 0 else pl.ds(RELAY, depth - RELAY)
        ref = gathered.at[y, (q_left, q_right)[way], part]
        return remote(ref, relay_send.at[way, t], relay_recv.at[way, t], (right, left)[way])

    def across(t, q):
        y = source_of(t)
        return remote(gathered.at[y, q], twin_send.at[t], twin_recv.at[t], twin)

    def bytes_of(t, sem):
        ref = gathered.at[source_of(t), pl.ds(0, RING)]
        return pltpu.make_async_copy(ref, ref, sem)

    def stage0(t):
        y = source_of(t)
        pltpu.make_async_copy(gathered.at[y, q_me], gathered.at[y, q_me], first_recv.at[y]).wait()
        side(t, 0).start()
        side(t, 1).start()
        across(t, q_me).start()

    def stage1(t):
        side(t, 0).wait_recv()
        relay(t, 0).start()
        side(t, 1).wait_recv()
        relay(t, 1).start()
        across(t, q_left).start()
        across(t, q_right).start()

    def stage2(t):
        relay(t, 0).wait_recv()
        relay(t, 1).wait_recv()
        across(t, q_far).start()

    for load in loads:
        load.wait()
    owned = owner_ref[...]
    sel = lax.broadcasted_iota(jnp.int32, (n_pair, tiles), 0) == owned
    sel_bf = one_hot_bf16(sel)
    count = jnp.zeros((n_pair, tiles), jnp.float32)
    span = 256
    for part in range(tiles // span):
        before = lax.broadcasted_iota(jnp.int32, (span, tiles), 0) + part * span < lax.broadcasted_iota(
            jnp.int32, (span, tiles), 1
        )
        count += jnp.dot(
            sel_bf[:, part * span : (part + 1) * span], one_hot_bf16(before), preferred_element_type=jnp.float32
        )
    base = (lax.broadcasted_iota(jnp.int32, (n_pair, tiles), 0) * per).astype(jnp.float32)
    rank = jnp.sum(jnp.where(sel, count + base, 0.0), axis=0, keepdims=True).astype(jnp.int32)

    flat = jnp.concatenate([amps_ref[o] for o in range(rows)], axis=1)
    for part in range(tiles // span):
        pick = one_hot_bf16(lax.broadcasted_iota(jnp.int32, (span, tiles), 0) + part * span == rank)
        got = jnp.dot(pick, flat, preferred_element_type=jnp.float32).astype(jnp.bfloat16)
        first = part * span // per
        for o in range(rows):
            send_a[first : first + span // per, o] = got[:, o * width : (o + 1) * width].reshape(
                span // per, per, width
            )

    def a_copy(i):
        to, there = spread_over(i)
        wanted = to - (pair - row_base) + lax.rem(there, RING) * CORES + there // RING
        return pltpu.make_async_remote_copy(
            src_ref=send_a.at[wanted],
            dst_ref=recv_a.at[spot],
            send_sem=a_send,
            recv_sem=a_recv,
            device_id=(to, there),
            device_id_type=MESH,
        )

    @pl.loop(1, n_pair)
    def _(i):
        a_copy(i).start()

    recv_a[spot] = send_a[served]

    def screen_copy(i):
        return pltpu.make_async_remote_copy(
            src_ref=coupling,
            dst_ref=coupling,
            send_sem=screen_send,
            recv_sem=screen_recv,
            device_id=(in_row(i), slab),
            device_id_type=MESH,
        )

    @pl.when(at_home)
    def _():
        coupling[...] = jnp.zeros_like(coupling)
        coupling[:, :per] = jnp.where(screen_ref[...] == 1, 1.0, 0.0)

        @pl.loop(1, ROW)
        def _(i):
            screen_copy(i).start()

    stage0(0)
    stage0(1)
    stage1(0)

    @pl.when(jnp.logical_not(at_home))
    def _():
        screen_copy(0).wait_recv()

    mine = one_hot_bf16(lax.broadcasted_iota(jnp.int32, (per, tiles), 0) + served * per == rank)
    classes = lax.broadcasted_iota(jnp.int32, (128, tiles), 0) == sym_ref[...]
    labels = lax.dot_general(
        mine, one_hot_bf16(classes), (((1,), (1,)), ((), ())), preferred_element_type=jnp.float32
    ).astype(jnp.bfloat16)
    same = lax.dot_general(labels, labels, (((1,), (1,)), ((), ())), preferred_element_type=jnp.float32)
    allowed = (coupling[:, :per] * same).astype(jnp.bfloat16)
    spread = one_hot_bf16(
        lax.broadcasted_iota(jnp.int32, (per, cols), 0) == lax.broadcasted_iota(jnp.int32, (per, cols), 1) // width
    )
    mask_ref[...] = jnp.dot(allowed, spread, preferred_element_type=jnp.float32)

    held = n_pair * rows

    def all_of(ref, sem):
        part = ref.at[pl.ds(0, n_pair - 1)]
        return pltpu.make_async_copy(part, part, sem)

    def arrange():
        all_of(recv_a, a_recv).wait()
        f32_buf[...] = recv_a[...].reshape(held * per, width).astype(jnp.float32)
        for k in range(per):
            a_mat[k // 2, :, (k % 2) * width : (k % 2 + 1) * width] = f32_buf[
                pl.ds(k, held, stride=per), :
            ].astype(jnp.bfloat16)

    def multiply(t):
        y = source_of(t)
        bytes_of(t, twin_recv.at[t]).wait()
        lhs = a_mat[y]
        for q in range(ROW):
            term = []
            for part in range(depth // width):
                row = mask_ref[pl.ds(y * (depth // width) + part, 1), q * piece : (q + 1) * piece]
                term.append(gathered[y, q, part * width : (part + 1) * width, :] * row.astype(jnp.bfloat16))
            prod = jnp.dot(lhs, jnp.concatenate(term, axis=0), preferred_element_type=jnp.float32)
            where = slice(q * piece, (q + 1) * piece)
            if t:
                prod = acc[:, where] + prod
            if t < n_slab - 1:
                acc[:, where] = prod
            else:
                for part in range(piece // width):
                    l = q * (piece // width) + part
                    f32_buf[pl.ds(l, held, stride=per), :] = prod[:, part * width : (part + 1) * width]

    for t in range(2, n_slab + 3):
        if t < n_slab:
            stage0(t)
        if t - 1 < n_slab:
            stage1(t - 1)
        if t - 2 < n_slab:
            stage2(t - 2)
        if t == 3:
            arrange()
        if t >= 3:
            multiply(t - 3)

    send_c[...] = f32_buf[...].astype(jnp.bfloat16).reshape(n_pair, rows, per, width)

    def c_copy(i):
        to = spread_over(i)
        return pltpu.make_async_remote_copy(
            src_ref=send_c.at[lax.rem(spot + i, n_pair)],
            dst_ref=out_ref.at[:, served],
            send_sem=c_send,
            recv_sem=c_recv,
            device_id=to,
            device_id_type=MESH,
        )

    @pl.loop(1, n_pair)
    def _(i):
        c_copy(i).start()

    out_ref[:, served] = send_c[spot]

    first_bytes = pltpu.make_async_copy(
        gathered.at[0, pl.ds(0, ROW - 1)], gathered.at[0, pl.ds(0, ROW - 1)], first_send
    )
    first_bytes.wait()

    @pl.when(jnp.logical_not(at_home))
    def _():
        pltpu.make_async_copy(gathered.at[0, 0], gathered.at[0, 0], first_send).wait()

    @pl.when(at_home)
    def _():
        @pl.loop(1, ROW)
        def _(i):
            screen_copy(i).wait_send()

    for t in range(n_slab):
        for way in range(2):
            side(t, way).wait_send()
            relay(t, way).wait_send()
        bytes_of(t, twin_send.at[t]).wait()
    all_of(send_a, a_send).wait()
    all_of(send_c, c_send).wait()
    all_of(send_c, c_recv).wait()


def on_device(amps, symmetry, screen, owner, integrals):
    n_pair, n_slab = lax.axis_size("pair"), lax.axis_size("slab")
    rows, tiles, width = amps.shape
    per = tiles // n_pair
    depth, cols = integrals.shape[1:]
    bf16 = jnp.bfloat16
    dma = pltpu.SemaphoreType.DMA
    return pl.pallas_call(
        functools.partial(kernel, n_pair, n_slab),
        out_shape=jax.ShapeDtypeStruct((rows, n_pair, per, width), bf16),
        in_specs=[pl.BlockSpec(memory_space=pl.ANY)] * 5,
        out_specs=pl.BlockSpec(memory_space=pltpu.VMEM),
        scratch_shapes=[
            pltpu.VMEM((1, tiles), jnp.int32),
            pltpu.VMEM((1, tiles), jnp.int32),
            pltpu.VMEM((per, per), jnp.int32),
            pltpu.VMEM((rows, tiles, width), bf16),
            pltpu.VMEM((n_pair, rows, per, width), bf16),
            pltpu.VMEM((n_pair, rows, per, width), bf16),
            pltpu.VMEM((n_slab, n_pair * rows, depth), bf16),
            pltpu.VMEM((n_pair * rows * per, width), jnp.float32),
            pltpu.VMEM((n_pair * rows, cols), jnp.float32),
            pltpu.VMEM((n_slab, ROW, depth, cols // ROW), bf16),
            pltpu.VMEM((per, 128), jnp.float32),
            pltpu.VMEM((per, cols), jnp.float32),
            pltpu.VMEM((n_pair, rows, per, width), bf16),
            dma((4,)),
            dma,
            dma((n_slab,)),
            dma((2, n_slab)),
            dma((2, n_slab)),
            dma((2, n_slab)),
            dma((2, n_slab)),
            dma((n_slab,)),
            dma((n_slab,)),
            dma,
            dma,
            dma,
            dma,
            dma,
            dma,
        ],
        compiler_params=pltpu.CompilerParams(
            collective_id=0, has_side_effects=True, vmem_limit_bytes=48 << 20
        ),
    )(owner[None, :], symmetry[None, :], screen[0], amps, integrals[0])


def solution(mesh):
    in_specs = (
        P(("pair", "slab"), None, None),
        P(),
        P("pair", None, None),
        P(),
        P("pair", "slab", None),
    )
    out_specs = P(("pair", "slab"), None, None, None)
    return jax.shard_map(
        on_device, mesh=mesh, in_specs=in_specs, out_specs=out_specs, check_vma=False
    )
```

```python
import functools

import jax
import jax.numpy as jnp
from jax import lax
from jax.experimental import pallas as pl
from jax.experimental.pallas import tpu as pltpu
from jax.sharding import PartitionSpec as P

MESH = pl.DeviceIdType.MESH
CORES = 2
RING = 4
ROW = CORES * RING
RELAY = 128
HALVES = 2
LAG = 7


def one_hot_bf16(cond):
    return jnp.where(cond, 1.0, 0.0).astype(jnp.bfloat16)


def kernel(
    n_pair,
    n_slab,
    owner_hbm,
    sym_hbm,
    screen_hbm,
    amps_hbm,
    b_hbm,
    out_ref,
    owner_ref,
    sym_ref,
    screen_ref,
    amps_ref,
    send_a,
    recv_a,
    a_mat,
    f32_a,
    f32_c,
    acc,
    spread_b,
    gathered,
    coupling,
    mask_ref,
    send_c,
    load_sem,
    x_send,
    x_recv,
    y_send,
    y_recv,
    side_send,
    side_recv,
    relay_send,
    relay_recv,
    twin_send,
    twin_recv,
    screen_send,
    screen_recv,
    a_send,
    a_recv,
    c_send,
    c_recv,
):
    pair = lax.axis_index("pair")
    slab = lax.axis_index("slab")
    rows, tiles, width = amps_hbm.shape
    per = tiles // n_pair
    depth, cols = b_hbm.shape
    half = cols // HALVES
    block = half // RING
    layer = pair // ROW
    ring = lax.rem(pair // CORES, RING)
    core = lax.rem(pair, CORES)
    row_base = layer * ROW

    home = ring + RING * core
    at_home = home == slab
    served = row_base + lax.rem(slab, RING) * CORES + slab // RING
    spot = layer * n_slab + slab

    loads = [
        pltpu.make_async_copy(src, dst, load_sem.at[i])
        for i, (src, dst) in enumerate(
            ((owner_hbm, owner_ref), (sym_hbm, sym_ref), (screen_hbm, screen_ref), (amps_hbm, amps_ref))
        )
    ]
    for load in loads:
        load.start()

    def device_at(x, c):
        return row_base + x * CORES + c

    def in_row(i):
        return row_base + lax.rem(pair - row_base + i, ROW)

    def spread_over(i):
        other = lax.rem(spot + i, n_pair)
        there = other // n_slab
        return there * ROW + pair - row_base, lax.rem(other, n_slab)

    twin = device_at(ring, 1 - core)
    right = device_at(lax.rem(ring + 1, RING), core)
    left = device_at(lax.rem(ring + RING - 1, RING), core)

    barrier = pltpu.get_barrier_semaphore()

    def greet(device):
        pl.semaphore_signal(barrier, inc=1, device_id=device, device_id_type=MESH)

    for i in range(1, ROW):
        greet((in_row(i), slab))
    for i in range(1, n_slab):
        greet((twin, lax.rem(slab + i, n_slab)))

    @pl.loop(1, n_pair)
    def _(i):
        greet(spread_over(i))

    pl.semaphore_wait(barrier, n_pair - 1 + ROW - 1 + n_slab - 1)

    def x_source(u, to):
        return b_hbm.at[:, pl.ds(pl.multiple_of(u * half + to * block, block), block)]

    def x_copy(u, i):
        to = lax.rem(ring + i, RING)
        return pltpu.make_async_remote_copy(
            src_ref=x_source(u, to),
            dst_ref=spread_b.at[u, ring],
            send_sem=x_send.at[u],
            recv_sem=x_recv.at[u, ring],
            device_id=(device_at(to, core), slab),
            device_id_type=MESH,
        )

    for u in range(HALVES):
        for i in (1, 3, 2):
            x_copy(u, i).start()
        pltpu.make_async_copy(x_source(u, ring), spread_b.at[u, ring], x_recv.at[u, ring]).start()

    def y_step(u):
        for i in range(RING):
            x0 = lax.rem(ring + i, RING)
            pltpu.make_async_copy(spread_b.at[u, x0], spread_b.at[u, x0], x_recv.at[u, x0]).wait()
            there = x0 + RING * core
            for swap in range(CORES):
                h = lax.rem(core + swap, CORES)
                src = spread_b.at[u, x0, :, pl.ds(pl.multiple_of(h * width, width), width)]
                dst = gathered.at[u, h, slab, ring]
                far = pltpu.make_async_remote_copy(
                    src_ref=src,
                    dst_ref=dst,
                    send_sem=y_send.at[u],
                    recv_sem=y_recv.at[u, slab],
                    device_id=(device_at(ring, h), there),
                    device_id_type=MESH,
                )
                if swap:
                    far.start()
                else:
                    near = pltpu.make_async_copy(src, dst, y_recv.at[u, slab])

                    @pl.when(there == slab)
                    def _():
                        near.start()

                    @pl.when(there != slab)
                    def _():
                        far.start()

    order = [0]
    for k in range(1, n_slab // 2):
        order += [k, n_slab - k]
    order += [n_slab // 2]

    def at(t):
        return t // n_slab, lax.rem(slab + order[t % n_slab], n_slab)

    def remote(ref, send, recv, to):
        return pltpu.make_async_remote_copy(
            src_ref=ref, dst_ref=ref, send_sem=send, recv_sem=recv, device_id=(to, slab), device_id_type=MESH
        )

    def side(t, way):
        u, y = at(t)
        ref = gathered.at[u, core, y, ring]
        return remote(ref, side_send.at[way, t], side_recv.at[way, t], (right, left)[way])

    def relay(t, way):
        u, y = at(t)
        x0 = lax.rem(ring + (RING - 1 if way == 0 else 1), RING)
        part = pl.ds(0, RELAY) if way == 0 else pl.ds(RELAY, depth - RELAY)
        ref = gathered.at[u, core, y, x0, part]
        return remote(ref, relay_send.at[way, t], relay_recv.at[way, t], (right, left)[way])

    def arrived_side(t, way):
        u, y = at(t)
        x0 = lax.rem(ring + (RING - 1 if way == 0 else 1), RING)
        ref = gathered.at[u, core, y, x0]
        return pltpu.make_async_copy(ref, ref, side_recv.at[way, t])

    def across(t):
        u, y = at(t)
        return remote(gathered.at[u, core, y], twin_send.at[t], twin_recv.at[t], twin)

    def stage0(t):
        u, y = at(t)
        ref = gathered.at[u, core, y, ring]
        pltpu.make_async_copy(ref, ref, y_recv.at[u, y]).wait()
        side(t, 0).start()
        side(t, 1).start()

    def stage1(t):
        arrived_side(t, 0).wait()
        relay(t, 0).start()
        arrived_side(t, 1).wait()
        relay(t, 1).start()

    def stage2(t):
        relay(t, 0).wait_recv()
        relay(t, 1).wait_recv()
        across(t).start()

    for load in loads:
        load.wait()
    owned = owner_ref[...]
    sel = lax.broadcasted_iota(jnp.int32, (n_pair, tiles), 0) == owned
    sel_bf = one_hot_bf16(sel)
    count = jnp.zeros((n_pair, tiles), jnp.float32)
    span = 256
    for part in range(tiles // span):
        before = lax.broadcasted_iota(jnp.int32, (span, tiles), 0) + part * span < lax.broadcasted_iota(
            jnp.int32, (span, tiles), 1
        )
        count += jnp.dot(
            sel_bf[:, part * span : (part + 1) * span], one_hot_bf16(before), preferred_element_type=jnp.float32
        )
    base = (lax.broadcasted_iota(jnp.int32, (n_pair, tiles), 0) * per).astype(jnp.float32)
    rank = jnp.sum(jnp.where(sel, count + base, 0.0), axis=0, keepdims=True).astype(jnp.int32)

    flat = jnp.concatenate([amps_ref[o] for o in range(rows)], axis=1)
    for part in range(tiles // span):
        pick = one_hot_bf16(lax.broadcasted_iota(jnp.int32, (span, tiles), 0) + part * span == rank)
        got = jnp.dot(pick, flat, preferred_element_type=jnp.float32).astype(jnp.bfloat16)
        first = part * span // per
        for o in range(rows):
            send_a[first : first + span // per, o] = got[:, o * width : (o + 1) * width].reshape(
                span // per, per, width
            )

    def a_copy(i):
        to, there = spread_over(i)
        wanted = to - (pair - row_base) + lax.rem(there, RING) * CORES + there // RING
        return pltpu.make_async_remote_copy(
            src_ref=send_a.at[wanted],
            dst_ref=recv_a.at[spot],
            send_sem=a_send,
            recv_sem=a_recv,
            device_id=(to, there),
            device_id_type=MESH,
        )

    y_step(0)

    @pl.loop(1, n_pair)
    def _(i):
        a_copy(i).start()

    y_step(1)
    recv_a[spot] = send_a[served]

    def screen_copy(i):
        return pltpu.make_async_remote_copy(
            src_ref=coupling,
            dst_ref=coupling,
            send_sem=screen_send,
            recv_sem=screen_recv,
            device_id=(in_row(i), slab),
            device_id_type=MESH,
        )

    @pl.when(at_home)
    def _():
        coupling[...] = jnp.zeros_like(coupling)
        coupling[:, :per] = jnp.where(screen_ref[...] == 1, 1.0, 0.0)

        @pl.loop(1, ROW)
        def _(i):
            screen_copy(i).start()

    @pl.when(jnp.logical_not(at_home))
    def _():
        screen_copy(0).wait_recv()

    mine = one_hot_bf16(lax.broadcasted_iota(jnp.int32, (per, tiles), 0) + served * per == rank)
    classes = lax.broadcasted_iota(jnp.int32, (128, tiles), 0) == sym_ref[...]
    labels = lax.dot_general(
        mine, one_hot_bf16(classes), (((1,), (1,)), ((), ())), preferred_element_type=jnp.float32
    ).astype(jnp.bfloat16)
    same = lax.dot_general(labels, labels, (((1,), (1,)), ((), ())), preferred_element_type=jnp.float32)
    allowed = (coupling[:, :per] * same).astype(jnp.bfloat16)
    spread = one_hot_bf16(
        lax.broadcasted_iota(jnp.int32, (per, cols), 0) == lax.broadcasted_iota(jnp.int32, (per, cols), 1) // width
    )
    mask_ref[...] = jnp.dot(allowed, spread, preferred_element_type=jnp.float32)

    held = n_pair * rows

    def all_of(ref, sem):
        part = ref.at[pl.ds(0, n_pair - 1)]
        return pltpu.make_async_copy(part, part, sem)

    def arrange():
        all_of(recv_a, a_recv).wait()
        f32_a[...] = recv_a[...].reshape(held * per, width).astype(jnp.float32)
        for k in range(per):
            a_mat[k // 2, :, (k % 2) * width : (k % 2 + 1) * width] = f32_a[
                pl.ds(k, held, stride=per), :
            ].astype(jnp.bfloat16)

    deep = depth // width
    part_l = per // HALVES

    def multiply(t):
        u, y = at(t)
        across(t).wait_recv()
        lhs = a_mat[y]
        for q in range(RING):
            start = u * half + q * block
            term = []
            for part in range(deep):
                row = mask_ref[pl.ds(y * deep + part, 1), start : start + block]
                span_k = slice(part * width, (part + 1) * width)
                both = jnp.concatenate([gathered[u, h, y, q, span_k, :] for h in range(CORES)], axis=1)
                term.append(both * row.astype(jnp.bfloat16))
            prod = jnp.dot(lhs, jnp.concatenate(term, axis=0), preferred_element_type=jnp.float32)
            where = slice(q * block, (q + 1) * block)
            k = t % n_slab
            if k:
                prod = acc[:, where] + prod
            if k < n_slab - 1:
                acc[:, where] = prod
            else:
                for h in range(CORES):
                    f32_c[pl.ds(q * CORES + h, held, stride=part_l), :] = prod[:, h * width : (h + 1) * width]

    def c_copy(u, i):
        return pltpu.make_async_remote_copy(
            src_ref=send_c.at[u, lax.rem(spot + i, n_pair)],
            dst_ref=out_ref.at[:, served, u],
            send_sem=c_send.at[u],
            recv_sem=c_recv.at[u],
            device_id=spread_over(i),
            device_id_type=MESH,
        )

    def give_back(u):
        send_c[u] = f32_c[...].astype(jnp.bfloat16).reshape(n_pair, rows, part_l, width)

        @pl.loop(1, n_pair)
        def _(i):
            c_copy(u, i).start()

        out_ref[:, served, u] = send_c[u, spot]

    steps = HALVES * n_slab
    done = 0
    for t in range(steps + 2):
        if t < steps:
            stage0(t)
        if 0 <= t - 1 < steps:
            stage1(t - 1)
        if 0 <= t - 2:
            stage2(t - 2)
        if t == LAG:
            arrange()
        if t >= LAG:
            for _ in range(2):
                if done <= t - 3:
                    multiply(done)
                    done += 1
                    if done % n_slab == 0:
                        give_back(done // n_slab - 1)
    while done < steps:
        multiply(done)
        done += 1
        if done % n_slab == 0:
            give_back(done // n_slab - 1)

    for u in range(HALVES):
        sent = spread_b.at[u, pl.ds(0, RING - 1)]
        pltpu.make_async_copy(sent, sent, x_send.at[u]).wait()
        some = gathered.at[u, 0, pl.ds(0, 1)]
        pltpu.make_async_copy(some, some, y_send.at[u]).wait()
        rest = gathered.at[u, 0, 0, pl.ds(0, RING - 1)]
        pltpu.make_async_copy(rest, rest, y_send.at[u]).wait()

    @pl.when(slab // RING != core)
    def _():
        for u in range(HALVES):
            one = gathered.at[u, 0, 0, 0]
            pltpu.make_async_copy(one, one, y_send.at[u]).wait()

    @pl.when(at_home)
    def _():
        @pl.loop(1, ROW)
        def _(i):
            screen_copy(i).wait_send()

    for t in range(steps):
        for way in range(2):
            side(t, way).wait_send()
            relay(t, way).wait_send()
        across(t).wait_send()
    all_of(send_a, a_send).wait()

    def result_bytes(u, sem):
        part = send_c.at[u, pl.ds(0, n_pair - 1)]
        return pltpu.make_async_copy(part, part, sem)

    for u in range(HALVES):
        result_bytes(u, c_send.at[u]).wait()
        result_bytes(u, c_recv.at[u]).wait()


def on_device(amps, symmetry, screen, owner, integrals):
    n_pair, n_slab = lax.axis_size("pair"), lax.axis_size("slab")
    rows, tiles, width = amps.shape
    per = tiles // n_pair
    depth, cols = integrals.shape[1:]
    block = cols // HALVES // RING
    held = n_pair * rows
    steps = HALVES * n_slab
    bf16, f32 = jnp.bfloat16, jnp.float32
    dma = pltpu.SemaphoreType.DMA
    result = pl.pallas_call(
        functools.partial(kernel, n_pair, n_slab),
        out_shape=jax.ShapeDtypeStruct((rows, n_pair, HALVES, per // HALVES, width), bf16),
        in_specs=[pl.BlockSpec(memory_space=pltpu.HBM)] * 5,
        out_specs=pl.BlockSpec(memory_space=pltpu.VMEM),
        scratch_shapes=[
            pltpu.VMEM((1, tiles), jnp.int32),
            pltpu.VMEM((1, tiles), jnp.int32),
            pltpu.VMEM((per, per), jnp.int32),
            pltpu.VMEM((rows, tiles, width), bf16),
            pltpu.VMEM((n_pair, rows, per, width), bf16),
            pltpu.VMEM((n_pair, rows, per, width), bf16),
            pltpu.VMEM((n_slab, held, depth), bf16),
            pltpu.VMEM((held * per, width), f32),
            pltpu.VMEM((held * per // HALVES, width), f32),
            pltpu.VMEM((held, cols // HALVES), f32),
            pltpu.VMEM((HALVES, RING, depth, block), bf16),
            pltpu.VMEM((HALVES, CORES, n_slab, RING, depth, block // CORES), bf16),
            pltpu.VMEM((per, 128), f32),
            pltpu.VMEM((per, cols), f32),
            pltpu.VMEM((HALVES, n_pair, rows, per // HALVES, width), bf16),
            dma((4,)),
            dma((HALVES,)),
            dma((HALVES, RING)),
            dma((HALVES,)),
            dma((HALVES, n_slab)),
            dma((2, steps)),
            dma((2, steps)),
            dma((2, steps)),
            dma((2, steps)),
            dma((steps,)),
            dma((steps,)),
            dma,
            dma,
            dma,
            dma,
            dma((HALVES,)),
            dma((HALVES,)),
        ],
        compiler_params=pltpu.CompilerParams(
            collective_id=0, has_side_effects=True, vmem_limit_bytes=63 << 20
        ),
    )(owner[None, :], symmetry[None, :], screen[0], amps, integrals[0])
    return result.reshape(rows, n_pair, per, width)


def solution(mesh):
    in_specs = (
        P(("pair", "slab"), None, None),
        P(),
        P("pair", None, None),
        P(),
        P("pair", "slab", None),
    )
    out_specs = P(("pair", "slab"), None, None, None)
    return jax.shard_map(
        on_device, mesh=mesh, in_specs=in_specs, out_specs=out_specs, check_vma=False
    )
```

```python
import functools

import jax
import jax.numpy as jnp
from jax import lax
from jax.experimental import pallas as pl
from jax.experimental.pallas import tpu as pltpu
from jax.sharding import PartitionSpec as P

MESH = pl.DeviceIdType.MESH
CORES = 2
RING = 4
ROW = CORES * RING
RELAY = 128
HALVES = 2
LAG = 11
AHEAD = 8
SIDE_LAG = 3
FAR_LAG = 6


def one_hot_bf16(cond):
    return jnp.where(cond, 1.0, 0.0).astype(jnp.bfloat16)


def kernel(
    n_pair,
    n_slab,
    owner_hbm,
    sym_hbm,
    screen_hbm,
    amps_hbm,
    b_hbm,
    out_ref,
    owner_ref,
    sym_ref,
    screen_ref,
    amps_ref,
    send_a,
    recv_a,
    a_mat,
    f32_a,
    f32_c,
    acc,
    spread_b,
    gathered,
    coupling,
    mask_ref,
    send_c,
    load_sem,
    x_send,
    x_recv,
    y_send,
    y_recv,
    side_send,
    side_recv,
    relay_send,
    relay_recv,
    twin_send,
    twin_recv,
    screen_send,
    screen_recv,
    a_send,
    a_recv,
    c_send,
    c_recv,
):
    pair = lax.axis_index("pair")
    slab = lax.axis_index("slab")
    rows, tiles, width = amps_hbm.shape
    per = tiles // n_pair
    depth, cols = b_hbm.shape
    half = cols // HALVES
    block = half // RING
    layer = pair // ROW
    ring = lax.rem(pair // CORES, RING)
    core = lax.rem(pair, CORES)
    row_base = layer * ROW

    home = ring + RING * core
    at_home = home == slab
    served = row_base + lax.rem(slab, RING) * CORES + slab // RING
    spot = layer * n_slab + slab

    loads = [
        pltpu.make_async_copy(src, dst, load_sem.at[i])
        for i, (src, dst) in enumerate(
            ((owner_hbm, owner_ref), (sym_hbm, sym_ref), (screen_hbm, screen_ref), (amps_hbm, amps_ref))
        )
    ]
    for load in loads:
        load.start()

    def device_at(x, c):
        return row_base + x * CORES + c

    def in_row(i):
        return row_base + lax.rem(pair - row_base + i, ROW)

    def spread_over(i):
        other = lax.rem(spot + i, n_pair)
        there = other // n_slab
        return there * ROW + pair - row_base, lax.rem(other, n_slab)

    twin = device_at(ring, 1 - core)
    right = device_at(lax.rem(ring + 1, RING), core)
    left = device_at(lax.rem(ring + RING - 1, RING), core)

    barrier = pltpu.get_barrier_semaphore()

    def greet(device):
        pl.semaphore_signal(barrier, inc=1, device_id=device, device_id_type=MESH)

    for i in range(1, ROW):
        greet((in_row(i), slab))
    for i in range(1, n_slab):
        greet((twin, lax.rem(slab + i, n_slab)))

    @pl.loop(1, n_pair)
    def _(i):
        greet(spread_over(i))

    pl.semaphore_wait(barrier, n_pair - 1 + ROW - 1 + n_slab - 1)

    def x_source(u, to):
        return b_hbm.at[:, pl.ds(pl.multiple_of(u * half + to * block, block), block)]

    def x_copy(u, i):
        to = lax.rem(ring + i, RING)
        return pltpu.make_async_remote_copy(
            src_ref=x_source(u, to),
            dst_ref=spread_b.at[u, ring],
            send_sem=x_send.at[u],
            recv_sem=x_recv.at[u, ring],
            device_id=(device_at(to, core), slab),
            device_id_type=MESH,
        )

    def x_step(u):
        for i in (1, 3, 2):
            x_copy(u, i).start()
        pltpu.make_async_copy(x_source(u, ring), spread_b.at[u, ring], x_recv.at[u, ring]).start()

    x_step(0)

    order = [0]
    for k in range(1, n_slab // 2):
        order += [k, n_slab - k]
    order += [n_slab // 2]

    def at(t):
        return t // n_slab, lax.rem(slab + order[t % n_slab], n_slab)

    def x_arrived(u):
        for x0 in range(RING):
            pltpu.make_async_copy(spread_b.at[u, x0], spread_b.at[u, x0], x_recv.at[u, x0]).wait()

    def y_step(t):
        u, k = t // n_slab, t % n_slab
        there = lax.rem(slab + n_slab - order[k], n_slab)

        @pl.when(there // RING == core)
        def _():
            for swap in range(CORES):
                h = lax.rem(core + swap, CORES)
                src = spread_b.at[u, lax.rem(there, RING), :, pl.ds(pl.multiple_of(h * width, width), width)]
                dst = gathered.at[u, h, slab, ring]
                if k == 0 and swap == 0:
                    pltpu.make_async_copy(src, dst, y_recv.at[u, slab]).start()
                else:
                    pltpu.make_async_remote_copy(
                        src_ref=src,
                        dst_ref=dst,
                        send_sem=y_send.at[u],
                        recv_sem=y_recv.at[u, slab],
                        device_id=(device_at(ring, h), there),
                        device_id_type=MESH,
                    ).start()

    def remote(ref, send, recv, to):
        return pltpu.make_async_remote_copy(
            src_ref=ref, dst_ref=ref, send_sem=send, recv_sem=recv, device_id=(to, slab), device_id_type=MESH
        )

    def side(t, way):
        u, y = at(t)
        ref = gathered.at[u, core, y, ring]
        return remote(ref, side_send.at[way, t], side_recv.at[way, t], (right, left)[way])

    def relay(t, way):
        u, y = at(t)
        x0 = lax.rem(ring + (RING - 1 if way == 0 else 1), RING)
        part = pl.ds(0, RELAY) if way == 0 else pl.ds(RELAY, depth - RELAY)
        ref = gathered.at[u, core, y, x0, part]
        return remote(ref, relay_send.at[way, t], relay_recv.at[way, t], (right, left)[way])

    def arrived_side(t, way):
        u, y = at(t)
        x0 = lax.rem(ring + (RING - 1 if way == 0 else 1), RING)
        ref = gathered.at[u, core, y, x0]
        return pltpu.make_async_copy(ref, ref, side_recv.at[way, t])

    def across(t):
        u, y = at(t)
        return remote(gathered.at[u, core, y], twin_send.at[t], twin_recv.at[t], twin)

    def stage0(t):
        u, y = at(t)
        ref = gathered.at[u, core, y, ring]
        pltpu.make_async_copy(ref, ref, y_recv.at[u, y]).wait()
        side(t, 0).start()
        side(t, 1).start()

    def stage1(t):
        arrived_side(t, 0).wait()
        relay(t, 0).start()
        arrived_side(t, 1).wait()
        relay(t, 1).start()

    def stage2(t):
        relay(t, 0).wait_recv()
        relay(t, 1).wait_recv()
        across(t).start()

    for load in loads:
        load.wait()
    owned = owner_ref[...]
    sel = lax.broadcasted_iota(jnp.int32, (n_pair, tiles), 0) == owned
    sel_bf = one_hot_bf16(sel)
    count = jnp.zeros((n_pair, tiles), jnp.float32)
    span = 256
    for part in range(tiles // span):
        before = lax.broadcasted_iota(jnp.int32, (span, tiles), 0) + part * span < lax.broadcasted_iota(
            jnp.int32, (span, tiles), 1
        )
        count += jnp.dot(
            sel_bf[:, part * span : (part + 1) * span], one_hot_bf16(before), preferred_element_type=jnp.float32
        )
    base = (lax.broadcasted_iota(jnp.int32, (n_pair, tiles), 0) * per).astype(jnp.float32)
    rank = jnp.sum(jnp.where(sel, count + base, 0.0), axis=0, keepdims=True).astype(jnp.int32)

    flat = jnp.concatenate([amps_ref[o] for o in range(rows)], axis=1)
    for part in range(tiles // span):
        pick = one_hot_bf16(lax.broadcasted_iota(jnp.int32, (span, tiles), 0) + part * span == rank)
        got = jnp.dot(pick, flat, preferred_element_type=jnp.float32).astype(jnp.bfloat16)
        first = part * span // per
        for o in range(rows):
            send_a[first : first + span // per, o] = got[:, o * width : (o + 1) * width].reshape(
                span // per, per, width
            )

    def a_copy(i):
        to, there = spread_over(i)
        wanted = to - (pair - row_base) + lax.rem(there, RING) * CORES + there // RING
        return pltpu.make_async_remote_copy(
            src_ref=send_a.at[wanted],
            dst_ref=recv_a.at[spot],
            send_sem=a_send,
            recv_sem=a_recv,
            device_id=(to, there),
            device_id_type=MESH,
        )

    @pl.loop(1, n_pair)
    def _(i):
        a_copy(i).start()

    x_arrived(0)
    for t in range(AHEAD):
        y_step(t)
    x_step(1)
    recv_a[spot] = send_a[served]

    def screen_copy(i):
        return pltpu.make_async_remote_copy(
            src_ref=coupling,
            dst_ref=coupling,
            send_sem=screen_send,
            recv_sem=screen_recv,
            device_id=(in_row(i), slab),
            device_id_type=MESH,
        )

    @pl.when(at_home)
    def _():
        coupling[...] = jnp.zeros_like(coupling)
        coupling[:, :per] = jnp.where(screen_ref[...] == 1, 1.0, 0.0)

        @pl.loop(1, ROW)
        def _(i):
            screen_copy(i).start()

    @pl.when(jnp.logical_not(at_home))
    def _():
        screen_copy(0).wait_recv()

    mine = one_hot_bf16(lax.broadcasted_iota(jnp.int32, (per, tiles), 0) + served * per == rank)
    classes = lax.broadcasted_iota(jnp.int32, (128, tiles), 0) == sym_ref[...]
    labels = lax.dot_general(
        mine, one_hot_bf16(classes), (((1,), (1,)), ((), ())), preferred_element_type=jnp.float32
    ).astype(jnp.bfloat16)
    same = lax.dot_general(labels, labels, (((1,), (1,)), ((), ())), preferred_element_type=jnp.float32)
    allowed = (coupling[:, :per] * same).astype(jnp.bfloat16)
    spread = one_hot_bf16(
        lax.broadcasted_iota(jnp.int32, (per, cols), 0) == lax.broadcasted_iota(jnp.int32, (per, cols), 1) // width
    )
    mask_ref[...] = jnp.dot(allowed, spread, preferred_element_type=jnp.float32)

    held = n_pair * rows

    def all_of(ref, sem):
        part = ref.at[pl.ds(0, n_pair - 1)]
        return pltpu.make_async_copy(part, part, sem)

    def arrange():
        all_of(recv_a, a_recv).wait()
        f32_a[...] = recv_a[...].reshape(held * per, width).astype(jnp.float32)
        for k in range(per):
            a_mat[k // 2, :, (k % 2) * width : (k % 2 + 1) * width] = f32_a[
                pl.ds(k, held, stride=per), :
            ].astype(jnp.bfloat16)

    deep = depth // width
    part_l = per // HALVES

    def multiply(t):
        u, y = at(t)
        across(t).wait_recv()
        lhs = a_mat[y]
        for q in range(RING):
            start = u * half + q * block
            term = []
            for part in range(deep):
                row = mask_ref[pl.ds(y * deep + part, 1), start : start + block]
                span_k = slice(part * width, (part + 1) * width)
                both = jnp.concatenate([gathered[u, h, y, q, span_k, :] for h in range(CORES)], axis=1)
                term.append(both * row.astype(jnp.bfloat16))
            prod = jnp.dot(lhs, jnp.concatenate(term, axis=0), preferred_element_type=jnp.float32)
            where = slice(q * block, (q + 1) * block)
            k = t % n_slab
            if k:
                prod = acc[:, where] + prod
            if k < n_slab - 1:
                acc[:, where] = prod
            else:
                for h in range(CORES):
                    f32_c[pl.ds(q * CORES + h, held, stride=part_l), :] = prod[:, h * width : (h + 1) * width]

    def c_copy(u, i):
        return pltpu.make_async_remote_copy(
            src_ref=send_c.at[u, lax.rem(spot + i, n_pair)],
            dst_ref=out_ref.at[:, served, u],
            send_sem=c_send.at[u],
            recv_sem=c_recv.at[u],
            device_id=spread_over(i),
            device_id_type=MESH,
        )

    def give_back(u):
        send_c[u] = f32_c[...].astype(jnp.bfloat16).reshape(n_pair, rows, part_l, width)

        @pl.loop(1, n_pair)
        def _(i):
            c_copy(u, i).start()

        out_ref[:, served, u] = send_c[u, spot]

    steps = HALVES * n_slab
    done = 0
    for t in range(steps + FAR_LAG):
        if t < steps:
            stage0(t)
        if t + AHEAD < steps:
            if t + AHEAD == n_slab:
                x_arrived(1)
            y_step(t + AHEAD)
        if 0 <= t - SIDE_LAG < steps:
            stage1(t - SIDE_LAG)
        if 0 <= t - FAR_LAG < steps:
            stage2(t - FAR_LAG)
        if t == LAG:
            arrange()
        if t >= LAG:
            for _ in range(2):
                if done < t - FAR_LAG:
                    multiply(done)
                    done += 1
                    if done % n_slab == 0:
                        give_back(done // n_slab - 1)
    while done < steps:
        multiply(done)
        done += 1
        if done % n_slab == 0:
            give_back(done // n_slab - 1)

    for u in range(HALVES):
        sent = spread_b.at[u, pl.ds(0, RING - 1)]
        pltpu.make_async_copy(sent, sent, x_send.at[u]).wait()
        some = gathered.at[u, 0, pl.ds(0, 1)]
        pltpu.make_async_copy(some, some, y_send.at[u]).wait()
        rest = gathered.at[u, 0, 0, pl.ds(0, RING - 1)]
        pltpu.make_async_copy(rest, rest, y_send.at[u]).wait()

    @pl.when(slab // RING != core)
    def _():
        for u in range(HALVES):
            one = gathered.at[u, 0, 0, 0]
            pltpu.make_async_copy(one, one, y_send.at[u]).wait()

    @pl.when(at_home)
    def _():
        @pl.loop(1, ROW)
        def _(i):
            screen_copy(i).wait_send()

    for t in range(steps):
        for way in range(2):
            side(t, way).wait_send()
            relay(t, way).wait_send()
        across(t).wait_send()
    all_of(send_a, a_send).wait()

    def result_bytes(u, sem):
        part = send_c.at[u, pl.ds(0, n_pair - 1)]
        return pltpu.make_async_copy(part, part, sem)

    for u in range(HALVES):
        result_bytes(u, c_send.at[u]).wait()
        result_bytes(u, c_recv.at[u]).wait()


def on_device(amps, symmetry, screen, owner, integrals):
    n_pair, n_slab = lax.axis_size("pair"), lax.axis_size("slab")
    rows, tiles, width = amps.shape
    per = tiles // n_pair
    depth, cols = integrals.shape[1:]
    block = cols // HALVES // RING
    held = n_pair * rows
    steps = HALVES * n_slab
    bf16, f32 = jnp.bfloat16, jnp.float32
    dma = pltpu.SemaphoreType.DMA
    result = pl.pallas_call(
        functools.partial(kernel, n_pair, n_slab),
        out_shape=jax.ShapeDtypeStruct((rows, n_pair, HALVES, per // HALVES, width), bf16),
        in_specs=[pl.BlockSpec(memory_space=pltpu.HBM)] * 5,
        out_specs=pl.BlockSpec(memory_space=pltpu.VMEM),
        scratch_shapes=[
            pltpu.VMEM((1, tiles), jnp.int32),
            pltpu.VMEM((1, tiles), jnp.int32),
            pltpu.VMEM((per, per), jnp.int32),
            pltpu.VMEM((rows, tiles, width), bf16),
            pltpu.VMEM((n_pair, rows, per, width), bf16),
            pltpu.VMEM((n_pair, rows, per, width), bf16),
            pltpu.VMEM((n_slab, held, depth), bf16),
            pltpu.VMEM((held * per, width), f32),
            pltpu.VMEM((held * per // HALVES, width), f32),
            pltpu.VMEM((held, cols // HALVES), f32),
            pltpu.VMEM((HALVES, RING, depth, block), bf16),
            pltpu.VMEM((HALVES, CORES, n_slab, RING, depth, block // CORES), bf16),
            pltpu.VMEM((per, 128), f32),
            pltpu.VMEM((per, cols), f32),
            pltpu.VMEM((HALVES, n_pair, rows, per // HALVES, width), bf16),
            dma((4,)),
            dma((HALVES,)),
            dma((HALVES, RING)),
            dma((HALVES,)),
            dma((HALVES, n_slab)),
            dma((2, steps)),
            dma((2, steps)),
            dma((2, steps)),
            dma((2, steps)),
            dma((steps,)),
            dma((steps,)),
            dma,
            dma,
            dma,
            dma,
            dma((HALVES,)),
            dma((HALVES,)),
        ],
        compiler_params=pltpu.CompilerParams(
            collective_id=0, has_side_effects=True, vmem_limit_bytes=63 << 20
        ),
    )(owner[None, :], symmetry[None, :], screen[0], amps, integrals[0])
    return result.reshape(rows, n_pair, per, width)


def solution(mesh):
    in_specs = (
        P(("pair", "slab"), None, None),
        P(),
        P("pair", None, None),
        P(),
        P("pair", "slab", None),
    )
    out_specs = P(("pair", "slab"), None, None, None)
    return jax.shard_map(
        on_device, mesh=mesh, in_specs=in_specs, out_specs=out_specs, check_vma=False
    )
```

```python
import functools

import jax
import jax.numpy as jnp
from jax import lax
from jax.experimental import pallas as pl
from jax.experimental.pallas import tpu as pltpu
from jax.sharding import PartitionSpec as P

MESH = pl.DeviceIdType.MESH
CORES = 2
RING = 4
ROW = CORES * RING
RELAY = 128
HALVES = 2
LAG = 11
FIRST = 8
ISSUE = {2: (8, 12), 5: (12, 16)}
SIDE_LAG = 3
FAR_LAG = 6


def one_hot_bf16(cond):
    return jnp.where(cond, 1.0, 0.0).astype(jnp.bfloat16)


def kernel(
    n_pair,
    n_slab,
    owner_hbm,
    sym_hbm,
    screen_hbm,
    amps_hbm,
    b_hbm,
    out_ref,
    owner_ref,
    sym_ref,
    screen_ref,
    amps_ref,
    send_a,
    recv_a,
    a_mat,
    f32_a,
    f32_c,
    acc,
    spread_b,
    gathered,
    coupling,
    mask_ref,
    send_c,
    load_sem,
    x_send,
    x_recv,
    y_send,
    y_recv,
    side_send,
    side_recv,
    relay_send,
    relay_recv,
    twin_send,
    twin_recv,
    screen_send,
    screen_recv,
    a_send,
    a_recv,
    c_send,
    c_recv,
):
    pair = lax.axis_index("pair")
    slab = lax.axis_index("slab")
    rows, tiles, width = amps_hbm.shape
    per = tiles // n_pair
    depth, cols = b_hbm.shape
    half = cols // HALVES
    block = half // RING
    layer = pair // ROW
    ring = lax.rem(pair // CORES, RING)
    core = lax.rem(pair, CORES)
    row_base = layer * ROW

    home = ring + RING * core
    at_home = home == slab
    served = row_base + lax.rem(slab, RING) * CORES + slab // RING
    spot = layer * n_slab + slab

    loads = [
        pltpu.make_async_copy(src, dst, load_sem.at[i])
        for i, (src, dst) in enumerate(
            ((owner_hbm, owner_ref), (sym_hbm, sym_ref), (screen_hbm, screen_ref), (amps_hbm, amps_ref))
        )
    ]
    for load in loads:
        load.start()

    def device_at(x, c):
        return row_base + x * CORES + c

    def in_row(i):
        return row_base + lax.rem(pair - row_base + i, ROW)

    def spread_over(i):
        other = lax.rem(spot + i, n_pair)
        there = other // n_slab
        return there * ROW + pair - row_base, lax.rem(other, n_slab)

    twin = device_at(ring, 1 - core)
    right = device_at(lax.rem(ring + 1, RING), core)
    left = device_at(lax.rem(ring + RING - 1, RING), core)

    barrier = pltpu.get_barrier_semaphore()

    def greet(device):
        pl.semaphore_signal(barrier, inc=1, device_id=device, device_id_type=MESH)

    for i in range(1, ROW):
        greet((in_row(i), slab))
    for i in range(1, n_slab):
        greet((twin, lax.rem(slab + i, n_slab)))

    @pl.loop(1, n_pair)
    def _(i):
        greet(spread_over(i))

    pl.semaphore_wait(barrier, n_pair - 1 + ROW - 1 + n_slab - 1)

    def x_source(u, to):
        return b_hbm.at[:, pl.ds(pl.multiple_of(u * half + to * block, block), block)]

    def x_copy(u, i):
        to = lax.rem(ring + i, RING)
        return pltpu.make_async_remote_copy(
            src_ref=x_source(u, to),
            dst_ref=spread_b.at[u, ring],
            send_sem=x_send.at[u],
            recv_sem=x_recv.at[u, ring],
            device_id=(device_at(to, core), slab),
            device_id_type=MESH,
        )

    def x_step(u):
        for i in (1, 3, 2):
            x_copy(u, i).start()
        pltpu.make_async_copy(x_source(u, ring), spread_b.at[u, ring], x_recv.at[u, ring]).start()

    x_step(0)

    order = [0]
    for k in range(1, n_slab // 2):
        order += [k, n_slab - k]
    order += [n_slab // 2]

    def at(t):
        return t // n_slab, lax.rem(slab + order[t % n_slab], n_slab)

    def x_arrived(u):
        for x0 in range(RING):
            pltpu.make_async_copy(spread_b.at[u, x0], spread_b.at[u, x0], x_recv.at[u, x0]).wait()

    def y_step(t):
        u, k = t // n_slab, t % n_slab
        there = lax.rem(slab + n_slab - order[k], n_slab)

        @pl.when(there // RING == core)
        def _():
            for swap in range(CORES):
                h = lax.rem(core + swap, CORES)
                src = spread_b.at[u, lax.rem(there, RING), :, pl.ds(pl.multiple_of(h * width, width), width)]
                dst = gathered.at[u, h, slab, ring]
                if k == 0 and swap == 0:
                    pltpu.make_async_copy(src, dst, y_recv.at[u, slab]).start()
                else:
                    pltpu.make_async_remote_copy(
                        src_ref=src,
                        dst_ref=dst,
                        send_sem=y_send.at[u],
                        recv_sem=y_recv.at[u, slab],
                        device_id=(device_at(ring, h), there),
                        device_id_type=MESH,
                    ).start()

    def remote(ref, send, recv, to):
        return pltpu.make_async_remote_copy(
            src_ref=ref, dst_ref=ref, send_sem=send, recv_sem=recv, device_id=(to, slab), device_id_type=MESH
        )

    def side(t, way):
        u, y = at(t)
        ref = gathered.at[u, core, y, ring]
        return remote(ref, side_send.at[way, t], side_recv.at[way, t], (right, left)[way])

    def relay(t, way):
        u, y = at(t)
        x0 = lax.rem(ring + (RING - 1 if way == 0 else 1), RING)
        part = pl.ds(0, RELAY) if way == 0 else pl.ds(RELAY, depth - RELAY)
        ref = gathered.at[u, core, y, x0, part]
        return remote(ref, relay_send.at[way, t], relay_recv.at[way, t], (right, left)[way])

    def arrived_side(t, way):
        u, y = at(t)
        x0 = lax.rem(ring + (RING - 1 if way == 0 else 1), RING)
        ref = gathered.at[u, core, y, x0]
        return pltpu.make_async_copy(ref, ref, side_recv.at[way, t])

    def across(t):
        u, y = at(t)
        return remote(gathered.at[u, core, y], twin_send.at[t], twin_recv.at[t], twin)

    def stage0(t):
        u, y = at(t)
        ref = gathered.at[u, core, y, ring]
        pltpu.make_async_copy(ref, ref, y_recv.at[u, y]).wait()
        side(t, 0).start()
        side(t, 1).start()

    def stage1(t):
        arrived_side(t, 0).wait()
        relay(t, 0).start()
        arrived_side(t, 1).wait()
        relay(t, 1).start()

    def stage2(t):
        relay(t, 0).wait_recv()
        relay(t, 1).wait_recv()
        across(t).start()

    for load in loads:
        load.wait()
    owned = owner_ref[...]
    sel = lax.broadcasted_iota(jnp.int32, (n_pair, tiles), 0) == owned
    sel_bf = one_hot_bf16(sel)
    count = jnp.zeros((n_pair, tiles), jnp.float32)
    span = 256
    for part in range(tiles // span):
        before = lax.broadcasted_iota(jnp.int32, (span, tiles), 0) + part * span < lax.broadcasted_iota(
            jnp.int32, (span, tiles), 1
        )
        count += jnp.dot(
            sel_bf[:, part * span : (part + 1) * span], one_hot_bf16(before), preferred_element_type=jnp.float32
        )
    base = (lax.broadcasted_iota(jnp.int32, (n_pair, tiles), 0) * per).astype(jnp.float32)
    rank = jnp.sum(jnp.where(sel, count + base, 0.0), axis=0, keepdims=True).astype(jnp.int32)

    flat = jnp.concatenate([amps_ref[o] for o in range(rows)], axis=1)
    for part in range(tiles // span):
        pick = one_hot_bf16(lax.broadcasted_iota(jnp.int32, (span, tiles), 0) + part * span == rank)
        got = jnp.dot(pick, flat, preferred_element_type=jnp.float32).astype(jnp.bfloat16)
        first = part * span // per
        for o in range(rows):
            send_a[first : first + span // per, o] = got[:, o * width : (o + 1) * width].reshape(
                span // per, per, width
            )

    def a_copy(i):
        to, there = spread_over(i)
        wanted = to - (pair - row_base) + lax.rem(there, RING) * CORES + there // RING
        return pltpu.make_async_remote_copy(
            src_ref=send_a.at[wanted],
            dst_ref=recv_a.at[spot],
            send_sem=a_send,
            recv_sem=a_recv,
            device_id=(to, there),
            device_id_type=MESH,
        )

    @pl.loop(1, n_pair)
    def _(i):
        a_copy(i).start()

    x_arrived(0)
    for t in range(FIRST):
        y_step(t)
    x_step(1)
    recv_a[spot] = send_a[served]

    def screen_copy(i):
        return pltpu.make_async_remote_copy(
            src_ref=coupling,
            dst_ref=coupling,
            send_sem=screen_send,
            recv_sem=screen_recv,
            device_id=(in_row(i), slab),
            device_id_type=MESH,
        )

    @pl.when(at_home)
    def _():
        coupling[...] = jnp.zeros_like(coupling)
        coupling[:, :per] = jnp.where(screen_ref[...] == 1, 1.0, 0.0)

        @pl.loop(1, ROW)
        def _(i):
            screen_copy(i).start()

    @pl.when(jnp.logical_not(at_home))
    def _():
        screen_copy(0).wait_recv()

    mine = one_hot_bf16(lax.broadcasted_iota(jnp.int32, (per, tiles), 0) + served * per == rank)
    classes = lax.broadcasted_iota(jnp.int32, (128, tiles), 0) == sym_ref[...]
    labels = lax.dot_general(
        mine, one_hot_bf16(classes), (((1,), (1,)), ((), ())), preferred_element_type=jnp.float32
    ).astype(jnp.bfloat16)
    same = lax.dot_general(labels, labels, (((1,), (1,)), ((), ())), preferred_element_type=jnp.float32)
    allowed = (coupling[:, :per] * same).astype(jnp.bfloat16)
    spread = one_hot_bf16(
        lax.broadcasted_iota(jnp.int32, (per, cols), 0) == lax.broadcasted_iota(jnp.int32, (per, cols), 1) // width
    )
    mask_ref[...] = jnp.dot(allowed, spread, preferred_element_type=jnp.float32)

    held = n_pair * rows

    def all_of(ref, sem):
        part = ref.at[pl.ds(0, n_pair - 1)]
        return pltpu.make_async_copy(part, part, sem)

    def arrange():
        all_of(recv_a, a_recv).wait()
        f32_a[...] = recv_a[...].reshape(held * per, width).astype(jnp.float32)
        for k in range(per):
            a_mat[k // 2, :, (k % 2) * width : (k % 2 + 1) * width] = f32_a[
                pl.ds(k, held, stride=per), :
            ].astype(jnp.bfloat16)

    deep = depth // width
    part_l = per // HALVES

    def multiply(t):
        u, y = at(t)
        across(t).wait_recv()
        lhs = a_mat[y]
        for q in range(RING):
            start = u * half + q * block
            term = []
            for part in range(deep):
                row = mask_ref[pl.ds(y * deep + part, 1), start : start + block]
                span_k = slice(part * width, (part + 1) * width)
                both = jnp.concatenate([gathered[u, h, y, q, span_k, :] for h in range(CORES)], axis=1)
                term.append(both * row.astype(jnp.bfloat16))
            prod = jnp.dot(lhs, jnp.concatenate(term, axis=0), preferred_element_type=jnp.float32)
            where = slice(q * block, (q + 1) * block)
            k = t % n_slab
            if k:
                prod = acc[:, where] + prod
            if k < n_slab - 1:
                acc[:, where] = prod
            else:
                for h in range(CORES):
                    f32_c[pl.ds(q * CORES + h, held, stride=part_l), :] = prod[:, h * width : (h + 1) * width]

    def c_copy(u, i):
        return pltpu.make_async_remote_copy(
            src_ref=send_c.at[u, lax.rem(spot + i, n_pair)],
            dst_ref=out_ref.at[:, served, u],
            send_sem=c_send.at[u],
            recv_sem=c_recv.at[u],
            device_id=spread_over(i),
            device_id_type=MESH,
        )

    def give_back(u):
        send_c[u] = f32_c[...].astype(jnp.bfloat16).reshape(n_pair, rows, part_l, width)

        @pl.loop(1, n_pair)
        def _(i):
            c_copy(u, i).start()

        out_ref[:, served, u] = send_c[u, spot]

    steps = HALVES * n_slab
    done = 0
    for t in range(steps + FAR_LAG):
        if t < steps:
            stage0(t)
        for r in range(*ISSUE.get(t, (0, 0))):
            if r == n_slab:
                x_arrived(1)
            y_step(r)
        if 0 <= t - SIDE_LAG < steps:
            stage1(t - SIDE_LAG)
        if 0 <= t - FAR_LAG < steps:
            stage2(t - FAR_LAG)
        if t == LAG:
            arrange()
        if t >= LAG:
            for _ in range(2):
                if done < t - FAR_LAG:
                    multiply(done)
                    done += 1
                    if done % n_slab == 0:
                        give_back(done // n_slab - 1)
    while done < steps:
        multiply(done)
        done += 1
        if done % n_slab == 0:
            give_back(done // n_slab - 1)

    for u in range(HALVES):
        sent = spread_b.at[u, pl.ds(0, RING - 1)]
        pltpu.make_async_copy(sent, sent, x_send.at[u]).wait()
        some = gathered.at[u, 0, pl.ds(0, 1)]
        pltpu.make_async_copy(some, some, y_send.at[u]).wait()
        rest = gathered.at[u, 0, 0, pl.ds(0, RING - 1)]
        pltpu.make_async_copy(rest, rest, y_send.at[u]).wait()

    @pl.when(slab // RING != core)
    def _():
        for u in range(HALVES):
            one = gathered.at[u, 0, 0, 0]
            pltpu.make_async_copy(one, one, y_send.at[u]).wait()

    @pl.when(at_home)
    def _():
        @pl.loop(1, ROW)
        def _(i):
            screen_copy(i).wait_send()

    for t in range(steps):
        for way in range(2):
            side(t, way).wait_send()
            relay(t, way).wait_send()
        across(t).wait_send()
    all_of(send_a, a_send).wait()

    def result_bytes(u, sem):
        part = send_c.at[u, pl.ds(0, n_pair - 1)]
        return pltpu.make_async_copy(part, part, sem)

    for u in range(HALVES):
        result_bytes(u, c_send.at[u]).wait()
        result_bytes(u, c_recv.at[u]).wait()


def on_device(amps, symmetry, screen, owner, integrals):
    n_pair, n_slab = lax.axis_size("pair"), lax.axis_size("slab")
    rows, tiles, width = amps.shape
    per = tiles // n_pair
    depth, cols = integrals.shape[1:]
    block = cols // HALVES // RING
    held = n_pair * rows
    steps = HALVES * n_slab
    bf16, f32 = jnp.bfloat16, jnp.float32
    dma = pltpu.SemaphoreType.DMA
    result = pl.pallas_call(
        functools.partial(kernel, n_pair, n_slab),
        out_shape=jax.ShapeDtypeStruct((rows, n_pair, HALVES, per // HALVES, width), bf16),
        in_specs=[pl.BlockSpec(memory_space=pltpu.HBM)] * 5,
        out_specs=pl.BlockSpec(memory_space=pltpu.VMEM),
        scratch_shapes=[
            pltpu.VMEM((1, tiles), jnp.int32),
            pltpu.VMEM((1, tiles), jnp.int32),
            pltpu.VMEM((per, per), jnp.int32),
            pltpu.VMEM((rows, tiles, width), bf16),
            pltpu.VMEM((n_pair, rows, per, width), bf16),
            pltpu.VMEM((n_pair, rows, per, width), bf16),
            pltpu.VMEM((n_slab, held, depth), bf16),
            pltpu.VMEM((held * per, width), f32),
            pltpu.VMEM((held * per // HALVES, width), f32),
            pltpu.VMEM((held, cols // HALVES), f32),
            pltpu.VMEM((HALVES, RING, depth, block), bf16),
            pltpu.VMEM((HALVES, CORES, n_slab, RING, depth, block // CORES), bf16),
            pltpu.VMEM((per, 128), f32),
            pltpu.VMEM((per, cols), f32),
            pltpu.VMEM((HALVES, n_pair, rows, per // HALVES, width), bf16),
            dma((4,)),
            dma((HALVES,)),
            dma((HALVES, RING)),
            dma((HALVES,)),
            dma((HALVES, n_slab)),
            dma((2, steps)),
            dma((2, steps)),
            dma((2, steps)),
            dma((2, steps)),
            dma((steps,)),
            dma((steps,)),
            dma,
            dma,
            dma,
            dma,
            dma((HALVES,)),
            dma((HALVES,)),
        ],
        compiler_params=pltpu.CompilerParams(
            collective_id=0, has_side_effects=True, vmem_limit_bytes=63 << 20
        ),
    )(owner[None, :], symmetry[None, :], screen[0], amps, integrals[0])
    return result.reshape(rows, n_pair, per, width)


def solution(mesh):
    in_specs = (
        P(("pair", "slab"), None, None),
        P(),
        P("pair", None, None),
        P(),
        P("pair", "slab", None),
    )
    out_specs = P(("pair", "slab"), None, None, None)
    return jax.shard_map(
        on_device, mesh=mesh, in_specs=in_specs, out_specs=out_specs, check_vma=False
    )
```
